32 devices in a mesh: dp: 8 (over z, core), tensor: 4 (over y, x).
Axes of the slice: x: 2, y: 2, z: 4, core: 2. Of those that a mesh axis runs over, the one named last changes fastest.
Arguments:
- tokens: bfloat16 [2048, 4096], P('dp', 'tensor'), may hold values from -6 to 6
- cotangent: bfloat16 [2048, 4096], P('dp', 'tensor'), may hold values from -6 to 6
- gate_weight: bfloat16 [4096, 14336], P('dp', 'tensor'), may hold values from -0.09375 to 0.09375
- up_weight: bfloat16 [4096, 14336], P('dp', 'tensor'), may hold values from -0.09375 to 0.09375
- down_weight: bfloat16 [14336, 4096], P('tensor', 'dp'), may hold values from -0.046875 to 0.046875
- counts: int32 [8], replicated, may hold values from 0 to 16, as said below
Outputs:
- outputs: bfloat16 [2048, 4096], P('dp', 'tensor')
- input_grads: bfloat16 [2048, 4096], P('dp', 'tensor')
The draws below stay inside these ranges and needn't reach their ends.
Inputs may be any that keep to these rules, and one draw needn't show every extreme that they name: counts[r] is the number of live 16-row blocks at the head of rank r's buffer; counts[r] + counts[(r + 4) % 8] = 16 for every rank r, some rank has 16 and some rank has 0.
All inputs are finite; a program needn't handle non-finite values.
Results may differ from the reference program's by a relative error of at most 0.005.
Values may be sent and summed in bfloat16 or wider, within the bound.
A program may use at most 192 MiB of HBM per device.

```python
import jax
import jax.numpy as jnp
from jax import lax

D = 4096
FF = 14336
BLOCK = 16
CAP_BLK = 16
ROWS = 2048
N_DP = 8


def draw_counts(key, part):
    moves = jax.random.randint(jax.random.fold_in(key, 12), (N_DP // 2,), -(CAP_BLK // 2), CAP_BLK // 2 + 1).astype(jnp.int32)
    moves = moves.at[0].set(CAP_BLK // 2)
    values = CAP_BLK // 2 + jnp.concatenate([moves, -moves])
    return values.astype(jnp.int32)


def block_levels(stream_key, extent, shards, low, high):
    def one(axis_at, parts):
        draws = jax.random.uniform(jax.random.fold_in(jax.random.fold_in(stream_key, 6), axis_at), (parts,), jnp.float32, low / len(shards), high / len(shards))
        return jnp.repeat(jnp.exp(draws), extent[axis_at] // parts).reshape((-1,) + (1,) * (len(extent) - axis_at - 1))

    gain = one(*shards[0])
    for cut in shards[1:]:
        gain = gain * one(*cut)
    return gain


def gaussian(rng, extent, deviation, limit, pieces=(), kind=jnp.bfloat16):
    result = deviation * jax.random.normal(rng, extent, jnp.float32)
    if pieces:
        result = result * block_levels(rng, extent, pieces, -0.22, 0.18)
    return jnp.clip(result, -limit, limit).astype(kind)


def setup_inputs(seed: int = 0) -> dict:
    seeds = jax.random.split(jax.random.key(seed), 7)
    return {
        "tokens": gaussian(seeds[0], (ROWS, D), 1.0, 6.0, ((0, 8), (1, 4))),
        "cotangent": gaussian(seeds[1], (ROWS, D), 1.0, 6.0, ((0, 8), (1, 4))),
        "gate_weight": gaussian(seeds[2], (D, FF), D ** -0.5, 0.09375, ((0, 8), (1, 4))),
        "up_weight": gaussian(seeds[3], (D, FF), D ** -0.5, 0.09375, ((0, 8), (1, 4))),
        "down_weight": gaussian(seeds[4], (FF, D), FF ** -0.5, 0.046875, ((0, 4), (1, 8))),
        "counts": draw_counts(jax.random.fold_in(seeds[6], 71), 0),
    }


def transposed(left, right):
    return lax.dot_general(left, right, (((1,), (1,)), ((), ())), preferred_element_type=jnp.float32)


def reference(tokens, cotangent, gate_weight, up_weight, down_weight, counts):
    block_ids = jnp.arange(CAP_BLK, dtype=jnp.int32)
    live_blocks = (block_ids[None, :] < counts[:, None]).astype(jnp.float32)
    row_mask = jnp.repeat(live_blocks, BLOCK, axis=1).reshape(N_DP * CAP_BLK * BLOCK, 1)
    gate_pre = jnp.dot(tokens, gate_weight, preferred_element_type=jnp.float32)
    up_pre = jnp.dot(tokens, up_weight, preferred_element_type=jnp.float32)
    sigmoid_gate = jax.nn.sigmoid(gate_pre)
    activated = gate_pre * sigmoid_gate
    hidden = (activated * up_pre).astype(jnp.bfloat16)
    outputs = (row_mask * jnp.dot(hidden, down_weight, preferred_element_type=jnp.float32)).astype(jnp.bfloat16)
    grad_hidden = transposed(cotangent, down_weight)
    grad_gate = (grad_hidden * up_pre * sigmoid_gate * (1.0 + gate_pre * (1.0 - sigmoid_gate))).astype(jnp.bfloat16)
    grad_up = (grad_hidden * activated).astype(jnp.bfloat16)
    summed = transposed(grad_gate, gate_weight) + transposed(grad_up, up_weight)
    input_grads = (row_mask * summed).astype(jnp.bfloat16)
    return outputs, input_grads
```

```python
import jax
import jax.numpy as jnp
from jax import lax
from jax.sharding import PartitionSpec as P

BLOCK = 16
CORES = 2


def transposed(left, right):
    return lax.dot_general(
        left, right, (((1,), (1,)), ((), ())), preferred_element_type=jnp.float32
    )


def matmul(left, right):
    return jnp.dot(left, right, preferred_element_type=jnp.float32)


def per_device(tokens, cotangent, gate_weight, up_weight, down_weight, counts):
    ranks = lax.axis_size("dp")
    tensors = lax.axis_size("tensor")
    chips = ranks // CORES
    half = chips // 2
    me = lax.axis_index("dp")
    core = me % CORES
    chip = me // CORES
    planes = [[z * CORES + c for z in range(chips)] for c in range(CORES)]
    rows, features = tokens.shape
    blocks = rows // BLOCK
    width, units = gate_weight.shape
    model = width * ranks
    part = units // chips

    def over_chips(pieces):
        return lax.all_to_all(pieces, "dp", 0, 0, tiled=True, axis_index_groups=planes)

    def swapped(block):
        return lax.ppermute(block, "dp", [(i, i ^ 1) for i in range(ranks)])

    both = jnp.concatenate([tokens, cotangent], axis=1)
    stacked = lax.all_gather(both, "dp", axis=0, tiled=True, axis_index_groups=planes)
    stacked = stacked.reshape(chips * blocks, BLOCK, 2 * features)
    slot = jnp.arange(blocks, dtype=jnp.int32)
    lower = jnp.arange(half, dtype=jnp.int32)
    lower_count = counts[lower * CORES + core][:, None]
    source = jnp.where(
        slot[None] < lower_count,
        lower[:, None] * blocks + slot[None],
        (lower[:, None] + half) * blocks + slot[None] - lower_count,
    ).reshape(-1)
    packed = jnp.take(stacked, source, axis=0).reshape(half * rows, 2 * features)
    work = half * rows
    whole_x = lax.all_gather(packed[:, :features], "tensor", axis=1, tiled=True)
    whole_dy = lax.all_gather(packed[:, features:], "tensor", axis=1, tiled=True)

    def by_core(whole):
        whole = whole.reshape(work, chips, CORES, width)
        zero, one = (whole[:, :, c].reshape(work, chips * width) for c in range(CORES))
        return jnp.where(core == 0, zero, one), jnp.where(core == 0, one, zero)

    x_own, x_far = by_core(whole_x)
    dy_own, dy_far = by_core(whole_dy)

    def rows_first(weight):
        pieces = weight.reshape(width, chips, part).transpose(1, 0, 2)
        return over_chips(pieces).reshape(chips * width, part)

    gate_own = rows_first(gate_weight)
    up_own = rows_first(up_weight)
    down_own = over_chips(down_weight.reshape(chips, part, width))
    gate_far, up_far, down_far = swapped(gate_own), swapped(up_own), swapped(down_own)

    def grad_in(left, right):
        left = left.reshape(work, chips, width)
        return lax.dot_general(
            left, right, (((1, 2), (0, 2)), ((), ())), preferred_element_type=jnp.float32
        )

    gate_pre = matmul(x_own, gate_own) + matmul(x_far, gate_far)
    up_pre = matmul(x_own, up_own) + matmul(x_far, up_far)
    sigmoid_gate = jax.nn.sigmoid(gate_pre)
    activated = gate_pre * sigmoid_gate
    hidden = (activated * up_pre).astype(jnp.bfloat16)
    grad_hidden = grad_in(dy_own, down_own) + grad_in(dy_far, down_far)
    grad_gate = (
        grad_hidden * up_pre * sigmoid_gate * (1.0 + gate_pre * (1.0 - sigmoid_gate))
    ).astype(jnp.bfloat16)
    grad_up = (grad_hidden * activated).astype(jnp.bfloat16)

    def out_part(down):
        result = lax.dot_general(
            hidden, down, (((1,), (1,)), ((), ())), preferred_element_type=jnp.float32
        )
        return result.astype(jnp.bfloat16).reshape(work, chips, width)

    def grad_part(gate, up):
        result = transposed(grad_gate, gate) + transposed(grad_up, up)
        return result.astype(jnp.bfloat16).reshape(work, chips, width)

    def whole_features(own, far):
        zero = jnp.where(core == 0, own, far)
        one = jnp.where(core == 0, far, own)
        return jnp.stack([zero, one], axis=2).reshape(work, model)

    def reduced(partial):
        pieces = partial.reshape(work, tensors, features).transpose(1, 0, 2)
        got = lax.all_to_all(pieces, "tensor", 0, 0, tiled=True)
        total = jnp.sum(got.astype(jnp.float32), axis=0).astype(jnp.bfloat16)
        pieces = total.reshape(half, 2, rows // 2, features).transpose(1, 0, 2, 3)
        pieces = pieces.reshape(chips, rows // 2, features)
        got = over_chips(pieces)
        return jnp.sum(got.astype(jnp.float32), axis=0).astype(jnp.bfloat16)

    out_rows = reduced(whole_features(out_part(down_own), out_part(down_far)))
    grad_rows = reduced(
        whole_features(grad_part(gate_own, up_own), grad_part(gate_far, up_far))
    )

    done = jnp.concatenate([out_rows, grad_rows], axis=1)
    route = [(i, (i + ranks // 2) % ranks) for i in range(ranks)]
    other = lax.ppermute(done, "dp", route)
    is_lower = chip < half
    pair = jnp.where(
        is_lower, jnp.concatenate([done, other]), jnp.concatenate([other, done])
    ).reshape(blocks, BLOCK, 2 * features)
    first = jnp.where(is_lower, 0, blocks - counts[me])
    home = jnp.take(pair, jnp.minimum(first + slot, blocks - 1), axis=0)
    home = jnp.where((slot < counts[me])[:, None, None], home, jnp.zeros_like(home))
    home = home.reshape(rows, 2 * features)
    return home[:, :features], home[:, features:]


def solution(mesh):
    in_specs = (
        P("dp", "tensor"),
        P("dp", "tensor"),
        P("dp", "tensor"),
        P("dp", "tensor"),
        P("tensor", "dp"),
        P(),
    )
    out_specs = (P("dp", "tensor"), P("dp", "tensor"))
    return jax.shard_map(
        per_device, mesh=mesh, in_specs=in_specs, out_specs=out_specs, check_vma=False
    )
```

```python
import jax
import jax.numpy as jnp
from jax import lax
from jax.sharding import PartitionSpec as P

BLOCK = 16
CORES = 2


def transposed(left, right):
    return lax.dot_general(
        left, right, (((1,), (1,)), ((), ())), preferred_element_type=jnp.float32
    )


def matmul(left, right):
    return jnp.dot(left, right, preferred_element_type=jnp.float32)


def per_device(tokens, cotangent, gate_weight, up_weight, down_weight, counts):
    ranks = lax.axis_size("dp")
    tensors = lax.axis_size("tensor")
    chips = ranks // CORES
    half = chips // 2
    me = lax.axis_index("dp")
    core = me % CORES
    chip = me // CORES
    rows, features = tokens.shape
    blocks = rows // BLOCK
    width, units = gate_weight.shape
    part = units // chips
    tensor = lax.axis_index("tensor")

    def to_chip(block, step):
        route = [(i, (i // CORES ^ step) * CORES + i % CORES) for i in range(ranks)]
        return lax.ppermute(block, "dp", route)

    def to_tensor(block, step):
        return lax.ppermute(block, "tensor", [(i, i ^ step) for i in range(tensors)])

    def swapped(block):
        return lax.ppermute(block, "dp", [(i, i ^ 1) for i in range(ranks)])

    both = jnp.concatenate([tokens, cotangent], axis=1)
    stacked = jnp.stack([both] + [to_chip(both, s) for s in range(1, chips)])
    stacked = stacked.reshape(chips * blocks, BLOCK, 2 * features)
    slot = jnp.arange(blocks, dtype=jnp.int32)
    lower = jnp.arange(half, dtype=jnp.int32)
    lower_count = counts[lower * CORES + core][:, None]
    source = jnp.where(
        slot[None] < lower_count,
        jnp.bitwise_xor(lower[:, None], chip) * blocks + slot[None],
        jnp.bitwise_xor(lower[:, None] + half, chip) * blocks + slot[None] - lower_count,
    ).reshape(-1)
    packed = jnp.take(stacked, source, axis=0).reshape(half * rows, 2 * features)
    work = half * rows
    whole_x = lax.all_gather(packed[:, :features], "tensor", axis=1, tiled=True)
    whole_dy = lax.all_gather(packed[:, features:], "tensor", axis=1, tiled=True)

    def by_core(whole):
        def slices(c):
            starts = [((chip ^ s) * CORES + c) * width for s in range(chips)]
            return jnp.concatenate(
                [lax.dynamic_slice_in_dim(whole, at, width, axis=1) for at in starts], axis=1
            )

        return slices(core), slices(1 - core)

    x_own, x_far = by_core(whole_x)
    dy_own, dy_far = by_core(whole_dy)

    def spread(piece):
        return [piece(chip)] + [to_chip(piece(chip ^ s), s) for s in range(1, chips)]

    def columns(weight):
        return lambda z: lax.dynamic_slice_in_dim(weight, z * part, part, axis=1)

    def down_rows(z):
        return lax.dynamic_slice_in_dim(down_weight, z * part, part, axis=0)

    def after(pieces, earlier):
        return lax.optimization_barrier((pieces, earlier))

    gate_pieces = spread(columns(gate_weight))
    up_pieces = spread(columns(up_weight))
    down_pieces = spread(down_rows)
    gate_own = jnp.concatenate(gate_pieces, axis=0)
    gate_far = swapped(gate_own)
    gate_pre = matmul(x_own, gate_own) + matmul(x_far, gate_far)
    up_pieces, gate_pre = after(up_pieces, gate_pre)
    up_own = jnp.concatenate(up_pieces, axis=0)
    up_far = swapped(up_own)
    up_pre = matmul(x_own, up_own) + matmul(x_far, up_far)
    sigmoid_gate = jax.nn.sigmoid(gate_pre)
    activated = gate_pre * sigmoid_gate
    hidden = (activated * up_pre).astype(jnp.bfloat16)
    down_pieces, hidden = after(down_pieces, hidden)
    down_own = jnp.concatenate(down_pieces, axis=1)
    down_far = swapped(down_own)
    grad_hidden = transposed(dy_own, down_own) + transposed(dy_far, down_far)
    grad_gate = (
        grad_hidden * up_pre * sigmoid_gate * (1.0 + gate_pre * (1.0 - sigmoid_gate))
    ).astype(jnp.bfloat16)
    grad_up = (grad_hidden * activated).astype(jnp.bfloat16)

    def out_part(down):
        return matmul(hidden, down).astype(jnp.bfloat16)

    def grad_part(gate, up):
        result = transposed(grad_gate, gate) + transposed(grad_up, up)
        return result.astype(jnp.bfloat16)

    def reduced(own, far):
        def piece(t):
            found = []
            for j in range(features // width):
                index = t * (features // width) + j
                at = (index // CORES ^ chip) * width
                here, there = (
                    lax.dynamic_slice_in_dim(side, at, width, axis=1) for side in (own, far)
                )
                found.append(jnp.where(index % CORES == core, here, there))
            return jnp.concatenate(found, axis=1)

        total = piece(tensor).astype(jnp.float32)
        for s in range(1, tensors):
            total += to_tensor(piece(tensor ^ s), s).astype(jnp.float32)
        pieces = total.reshape(half, 2, rows // 2, features)

        def chunk(z):
            return pieces[z % half, z // half]

        total = chunk(chip)
        for s in range(1, chips):
            sent = chunk(chip ^ s).astype(jnp.bfloat16)
            total += to_chip(sent, s).astype(jnp.float32)
        return total.astype(jnp.bfloat16)

    out_rows = reduced(out_part(down_own), out_part(down_far))
    grad_rows = reduced(grad_part(gate_own, up_own), grad_part(gate_far, up_far))

    is_lower = chip < half
    first = jnp.where(is_lower, 0, blocks - counts[me])

    def home(done):
        other = to_chip(done, half)
        pair = jnp.where(
            is_lower, jnp.concatenate([done, other]), jnp.concatenate([other, done])
        ).reshape(blocks, BLOCK, features)
        mine = jnp.take(pair, jnp.minimum(first + slot, blocks - 1), axis=0)
        mine = jnp.where((slot < counts[me])[:, None, None], mine, jnp.zeros_like(mine))
        return mine.reshape(rows, features)

    return home(out_rows), home(grad_rows)


def solution(mesh):
    in_specs = (
        P("dp", "tensor"),
        P("dp", "tensor"),
        P("dp", "tensor"),
        P("dp", "tensor"),
        P("tensor", "dp"),
        P(),
    )
    out_specs = (P("dp", "tensor"), P("dp", "tensor"))
    return jax.shard_map(
        per_device, mesh=mesh, in_specs=in_specs, out_specs=out_specs, check_vma=False
    )
```

```python
import functools

import jax
import jax.numpy as jnp
from jax import lax
from jax.experimental import pallas as pl
from jax.experimental.pallas import tpu as pltpu
from jax.sharding import PartitionSpec as P

BLOCK = 16
CORES = 2


def transposed(left, right):
    return lax.dot_general(
        left, right, (((1,), (1,)), ((), ())), preferred_element_type=jnp.float32
    )


def matmul(left, right):
    return jnp.dot(left, right, preferred_element_type=jnp.float32)


def spread_kernel(sizes, rows, gate, up, down, *refs):
    chips, tensors, part, width = sizes
    rows_all, own, far = refs[0], refs[1:4], refs[4:7]
    send, recv, local = refs[7:]
    me = lax.axis_index("dp")
    tensor = lax.axis_index("tensor")
    core, chip = me % CORES, me // CORES
    sibling = (me + 1 - 2 * core, tensor)

    def xored(value, step, size):
        result, bit = 0, 1
        while bit < size:
            digit = value // bit % 2
            result += (1 - digit if step & bit else digit) * bit
            bit *= 2
        return result

    def chip_of(step):
        return xored(chip, step, chips)

    def at_chip(step):
        return (chip_of(step) * CORES + core, tensor)

    def at_tensor(step):
        return (me, xored(tensor, step, tensors))

    steps = list(range(chips // 2, chips)) + list(range(1, chips // 2))
    peers = [at_chip(s) for s in steps] + [at_tensor(j) for j in range(1, tensors)] + [sibling]
    barrier = pltpu.get_barrier_semaphore()
    for peer in peers:
        pl.semaphore_signal(
            barrier, inc=1, device_id=peer, device_id_type=pl.DeviceIdType.MESH
        )
    pl.semaphore_wait(barrier, len(peers))

    started = []

    def put(source, target, device):
        n = len(started)
        copy = pltpu.make_async_remote_copy(
            src_ref=source,
            dst_ref=target,
            send_sem=send.at[n],
            recv_sem=recv.at[n],
            device_id=device,
            device_id_type=pl.DeviceIdType.MESH,
        )
        copy.start()
        started.append(copy)
        return copy

    def cut(ref, z, axis):
        if len(ref.shape) == 3:
            return ref.at[z]
        span = pl.ds(pl.multiple_of(z * part, part), part)
        return ref.at[span, :] if axis == 0 else ref.at[:, span]

    def slot(ref, s, axis):
        return ref.at[:, pl.ds(s * width, width)] if axis == 0 else ref.at[s]

    weights = [(gate, own[0], far[0], 1), (up, own[1], far[1], 1), (down, own[2], far[2], 0)]
    arriving_rows = [(s, put(rows, rows_all.at[0, s], at_chip(s))) for s in steps]
    arriving = []
    for weight, mine, other, axis in weights:
        for s in steps:
            copy = put(cut(weight, chip_of(s), axis), slot(mine, s, axis), at_chip(s))
            arriving.append((copy, slot(mine, s, axis), slot(other, s, axis)))
    here = [pltpu.make_async_copy(rows, rows_all.at[0, 0], local.at[0])]
    last = []
    for j in range(1, tensors):
        last.append(put(rows, rows_all.at[j, 0], at_tensor(j)))
    for n, (weight, mine, other, axis) in enumerate(weights):
        piece = cut(weight, chip, axis)
        here.append(pltpu.make_async_copy(piece, slot(mine, 0, axis), local.at[n + 1]))
        last.append(put(piece, slot(other, 0, axis), sibling))
    for copy in here:
        copy.start()
    for s, copy in arriving_rows:
        copy.wait_recv()
        for j in range(1, tensors):
            last.append(put(rows_all.at[0, s], rows_all.at[j, s], at_tensor(j)))
    for copy, mine, other in arriving:
        copy.wait_recv()
        last.append(put(mine, other, sibling))
    for copy in last:
        copy.wait_recv()
    for copy in started:
        copy.wait_send()
    for copy in here:
        copy.wait()


def spread(rows, gate, up, down, sizes):
    chips, tensors, part, width = sizes
    kind = gate.dtype
    side = jax.ShapeDtypeStruct((chips, width, part), kind)
    across = jax.ShapeDtypeStruct((part, chips * width), kind)
    copies = 4 * (chips - 1) + chips * (tensors - 1) + 3 * chips
    anywhere = pl.BlockSpec(memory_space=pl.ANY)
    return pl.pallas_call(
        functools.partial(spread_kernel, sizes),
        out_shape=[
            jax.ShapeDtypeStruct((tensors, chips) + rows.shape, kind),
            side, side, across, side, side, across,
        ],
        in_specs=[anywhere] * 4,
        out_specs=[anywhere] * 7,
        scratch_shapes=[
            pltpu.SemaphoreType.DMA((copies,)),
            pltpu.SemaphoreType.DMA((copies,)),
            pltpu.SemaphoreType.DMA((4,)),
        ],
        compiler_params=pltpu.CompilerParams(collective_id=0, has_side_effects=True),
    )(rows, gate, up, down)


def per_device(tokens, cotangent, gate_weight, up_weight, down_weight, counts):
    ranks = lax.axis_size("dp")
    tensors = lax.axis_size("tensor")
    chips = ranks // CORES
    half = chips // 2
    me = lax.axis_index("dp")
    core = me % CORES
    chip = me // CORES
    rows, features = tokens.shape
    blocks = rows // BLOCK
    width, units = gate_weight.shape
    part = units // chips
    tensor = lax.axis_index("tensor")

    def to_chip(block, step):
        route = [(i, (i // CORES ^ step) * CORES + i % CORES) for i in range(ranks)]
        return lax.ppermute(block, "dp", route)

    def to_tensor(block, step):
        return lax.ppermute(block, "tensor", [(i, i ^ step) for i in range(tensors)])

    def pieces_of(weight):
        if part % 128 == 0:
            return weight
        return weight.reshape(width, chips, part).transpose(1, 0, 2)

    both = jnp.concatenate([tokens, cotangent], axis=1)
    raw, gate_own, up_own, down_own, gate_far, up_far, down_far = spread(
        both, pieces_of(gate_weight), pieces_of(up_weight), down_weight, (chips, tensors, part, width)
    )
    gate_own, up_own, gate_far, up_far = (
        w.reshape(chips * width, part) for w in (gate_own, up_own, gate_far, up_far)
    )

    slot = jnp.arange(blocks, dtype=jnp.int32)
    lower = jnp.arange(half, dtype=jnp.int32)
    lower_count = counts[lower * CORES + core][:, None]
    source = jnp.where(
        slot[None] < lower_count,
        jnp.bitwise_xor(lower[:, None], chip) * blocks + slot[None],
        jnp.bitwise_xor(lower[:, None] + half, chip) * blocks + slot[None] - lower_count,
    ).reshape(-1)
    work = half * rows
    raw = raw.reshape(tensors, chips * blocks, BLOCK, 2 * features)
    packed = jnp.take(raw, source, axis=1).reshape(tensors, work, 2 * features)

    def slices(c, shift):
        found = []
        for s in range(chips):
            at = ((chip ^ s) * CORES + c) * width
            start = (at // features ^ tensor, 0, at % features + shift)
            found.append(lax.dynamic_slice(packed, start, (1, work, width))[0])
        return jnp.concatenate(found, axis=1)

    x_own, x_far = slices(core, 0), slices(1 - core, 0)
    dy_own, dy_far = slices(core, features), slices(1 - core, features)
    gate_pre = matmul(x_own, gate_own) + matmul(x_far, gate_far)
    up_pre = matmul(x_own, up_own) + matmul(x_far, up_far)
    sigmoid_gate = jax.nn.sigmoid(gate_pre)
    activated = gate_pre * sigmoid_gate
    hidden = (activated * up_pre).astype(jnp.bfloat16)
    grad_hidden = transposed(dy_own, down_own) + transposed(dy_far, down_far)
    grad_gate = (
        grad_hidden * up_pre * sigmoid_gate * (1.0 + gate_pre * (1.0 - sigmoid_gate))
    ).astype(jnp.bfloat16)
    grad_up = (grad_hidden * activated).astype(jnp.bfloat16)

    def out_part(down):
        return matmul(hidden, down).astype(jnp.bfloat16)

    def grad_part(gate, up):
        result = transposed(grad_gate, gate) + transposed(grad_up, up)
        return result.astype(jnp.bfloat16)

    def reduced(own, far):
        def piece(t):
            found = []
            for j in range(features // width):
                index = t * (features // width) + j
                at = (index // CORES ^ chip) * width
                here, there = (
                    lax.dynamic_slice_in_dim(side, at, width, axis=1) for side in (own, far)
                )
                found.append(jnp.where(index % CORES == core, here, there))
            return jnp.concatenate(found, axis=1)

        total = piece(tensor).astype(jnp.float32)
        for s in range(1, tensors):
            total += to_tensor(piece(tensor ^ s), s).astype(jnp.float32)
        pieces = total.reshape(half, 2, rows // 2, features)

        def chunk(z):
            return pieces[z % half, z // half]

        total = chunk(chip)
        for s in range(1, chips):
            sent = chunk(chip ^ s).astype(jnp.bfloat16)
            total += to_chip(sent, s).astype(jnp.float32)
        return total.astype(jnp.bfloat16)

    out_rows = reduced(out_part(down_own), out_part(down_far))
    grad_rows = reduced(grad_part(gate_own, up_own), grad_part(gate_far, up_far))

    is_lower = chip < half
    first = jnp.where(is_lower, 0, blocks - counts[me])

    def home(done):
        other = to_chip(done, half)
        pair = jnp.where(
            is_lower, jnp.concatenate([done, other]), jnp.concatenate([other, done])
        ).reshape(blocks, BLOCK, features)
        mine = jnp.take(pair, jnp.minimum(first + slot, blocks - 1), axis=0)
        mine = jnp.where((slot < counts[me])[:, None, None], mine, jnp.zeros_like(mine))
        return mine.reshape(rows, features)

    return home(out_rows), home(grad_rows)


def solution(mesh):
    in_specs = (
        P("dp", "tensor"),
        P("dp", "tensor"),
        P("dp", "tensor"),
        P("dp", "tensor"),
        P("tensor", "dp"),
        P(),
    )
    out_specs = (P("dp", "tensor"), P("dp", "tensor"))
    return jax.shard_map(
        per_device, mesh=mesh, in_specs=in_specs, out_specs=out_specs, check_vma=False
    )
```

```python
import functools

import jax
import jax.numpy as jnp
from jax import lax
from jax.experimental import pallas as pl
from jax.experimental.pallas import tpu as pltpu
from jax.sharding import PartitionSpec as P

BLOCK = 16
CORES = 2


def transposed(left, right):
    return lax.dot_general(
        left, right, (((1,), (1,)), ((), ())), preferred_element_type=jnp.float32
    )


def matmul(left, right):
    return jnp.dot(left, right, preferred_element_type=jnp.float32)


def spread_kernel(sizes, rows, gate, up, *refs):
    chips, tensors, part, width = sizes
    rows_all, own, far = refs[0], refs[1:3], refs[3:5]
    send, recv, local = refs[5:]
    me = lax.axis_index("dp")
    tensor = lax.axis_index("tensor")
    core, chip = me % CORES, me // CORES
    sibling = (me + 1 - 2 * core, tensor)

    def xored(value, step, size):
        result, bit = 0, 1
        while bit < size:
            digit = value // bit % 2
            result += (1 - digit if step & bit else digit) * bit
            bit *= 2
        return result

    def chip_of(step):
        return xored(chip, step, chips)

    def at_chip(step):
        return (chip_of(step) * CORES + core, tensor)

    def at_tensor(step):
        return (me, xored(tensor, step, tensors))

    steps = list(range(chips // 2, chips)) + list(range(1, chips // 2))
    peers = [at_chip(s) for s in steps] + [at_tensor(j) for j in range(1, tensors)] + [sibling]
    barrier = pltpu.get_barrier_semaphore()
    for peer in peers:
        pl.semaphore_signal(
            barrier, inc=1, device_id=peer, device_id_type=pl.DeviceIdType.MESH
        )
    pl.semaphore_wait(barrier, len(peers))

    started = []

    def put(source, target, device):
        n = len(started)
        copy = pltpu.make_async_remote_copy(
            src_ref=source,
            dst_ref=target,
            send_sem=send.at[n],
            recv_sem=recv.at[n],
            device_id=device,
            device_id_type=pl.DeviceIdType.MESH,
        )
        copy.start()
        started.append(copy)
        return copy

    def cut(ref, z):
        if len(ref.shape) == 3:
            return ref.at[z]
        return ref.at[:, pl.ds(pl.multiple_of(z * part, part), part)]

    weights = [(gate, own[0], far[0]), (up, own[1], far[1])]
    arriving_rows = [(s, put(rows, rows_all.at[0, s], at_chip(s))) for s in steps]
    arriving = []
    for weight, mine, other in weights:
        for s in steps:
            copy = put(cut(weight, chip_of(s)), mine.at[s], at_chip(s))
            arriving.append((copy, mine.at[s], other.at[s]))
    here = [pltpu.make_async_copy(rows, rows_all.at[0, 0], local.at[0])]
    last = []
    for j in range(1, tensors):
        last.append(put(rows, rows_all.at[j, 0], at_tensor(j)))
    for n, (weight, mine, other) in enumerate(weights):
        piece = cut(weight, chip)
        here.append(pltpu.make_async_copy(piece, mine.at[0], local.at[n + 1]))
        last.append(put(piece, other.at[0], sibling))
    for copy in here:
        copy.start()
    for s, copy in arriving_rows:
        copy.wait_recv()
        for j in range(1, tensors):
            last.append(put(rows_all.at[0, s], rows_all.at[j, s], at_tensor(j)))
    for copy, mine, other in arriving:
        copy.wait_recv()
        last.append(put(mine, other, sibling))
    for copy in last:
        copy.wait_recv()
    for copy in started:
        copy.wait_send()
    for copy in here:
        copy.wait()


def spread(rows, gate, up, sizes):
    chips, tensors, part, width = sizes
    kind = gate.dtype
    side = jax.ShapeDtypeStruct((chips, width, part), kind)
    copies = 3 * (chips - 1) + chips * (tensors - 1) + 2 * chips
    anywhere = pl.BlockSpec(memory_space=pl.ANY)
    return pl.pallas_call(
        functools.partial(spread_kernel, sizes),
        out_shape=[
            jax.ShapeDtypeStruct((tensors, chips) + rows.shape, kind),
            side, side, side, side,
        ],
        in_specs=[anywhere] * 3,
        out_specs=[anywhere] * 5,
        scratch_shapes=[
            pltpu.SemaphoreType.DMA((copies,)),
            pltpu.SemaphoreType.DMA((copies,)),
            pltpu.SemaphoreType.DMA((3,)),
        ],
        compiler_params=pltpu.CompilerParams(collective_id=0, has_side_effects=True),
    )(rows, gate, up)


def per_device(tokens, cotangent, gate_weight, up_weight, down_weight, counts):
    ranks = lax.axis_size("dp")
    tensors = lax.axis_size("tensor")
    chips = ranks // CORES
    half = chips // 2
    me = lax.axis_index("dp")
    core = me % CORES
    chip = me // CORES
    rows, features = tokens.shape
    blocks = rows // BLOCK
    width, units = gate_weight.shape
    part = units // chips
    tensor = lax.axis_index("tensor")

    def to_chip(block, step):
        route = [(i, (i // CORES ^ step) * CORES + i % CORES) for i in range(ranks)]
        return lax.ppermute(block, "dp", route)

    def swapped(block):
        return lax.ppermute(block, "dp", [(i, i ^ 1) for i in range(ranks)])

    def to_tensor(block, step):
        return lax.ppermute(block, "tensor", [(i, i ^ step) for i in range(tensors)])

    def pieces_of(weight):
        if part % 128 == 0:
            return weight
        return weight.reshape(width, chips, part).transpose(1, 0, 2)

    both = jnp.concatenate([tokens, cotangent], axis=1)
    raw, gate_own, up_own, gate_far, up_far = spread(
        both, pieces_of(gate_weight), pieces_of(up_weight), (chips, tensors, part, width)
    )
    down_weight, raw = lax.optimization_barrier((down_weight, raw))

    def down_rows(z):
        return lax.dynamic_slice_in_dim(down_weight, z * part, part, axis=0)

    down_pieces = [to_chip(down_rows(chip ^ s), s) for s in range(1, chips)]
    gate_own, up_own, gate_far, up_far = (
        w.reshape(chips * width, part) for w in (gate_own, up_own, gate_far, up_far)
    )

    slot = jnp.arange(blocks, dtype=jnp.int32)
    lower = jnp.arange(half, dtype=jnp.int32)
    lower_count = counts[lower * CORES + core][:, None]
    source = jnp.where(
        slot[None] < lower_count,
        jnp.bitwise_xor(lower[:, None], chip) * blocks + slot[None],
        jnp.bitwise_xor(lower[:, None] + half, chip) * blocks + slot[None] - lower_count,
    ).reshape(-1)
    work = half * rows
    raw = raw.reshape(tensors, chips * blocks, BLOCK, 2 * features)
    packed = jnp.take(raw, source, axis=1).reshape(tensors, work, 2 * features)

    def slices(c, shift):
        found = []
        for s in range(chips):
            at = ((chip ^ s) * CORES + c) * width
            start = (at // features ^ tensor, 0, at % features + shift)
            found.append(lax.dynamic_slice(packed, start, (1, work, width))[0])
        return jnp.concatenate(found, axis=1)

    x_own, x_far = slices(core, 0), slices(1 - core, 0)
    dy_own, dy_far = slices(core, features), slices(1 - core, features)
    gate_pre = matmul(x_own, gate_own) + matmul(x_far, gate_far)
    up_pre = matmul(x_own, up_own) + matmul(x_far, up_far)
    sigmoid_gate = jax.nn.sigmoid(gate_pre)
    activated = gate_pre * sigmoid_gate
    hidden = (activated * up_pre).astype(jnp.bfloat16)
    down_pieces, hidden = lax.optimization_barrier((down_pieces, hidden))
    down_own = jnp.concatenate([down_rows(chip)] + list(down_pieces), axis=1)
    down_far = swapped(down_own)
    grad_hidden = transposed(dy_own, down_own) + transposed(dy_far, down_far)
    grad_gate = (
        grad_hidden * up_pre * sigmoid_gate * (1.0 + gate_pre * (1.0 - sigmoid_gate))
    ).astype(jnp.bfloat16)
    grad_up = (grad_hidden * activated).astype(jnp.bfloat16)

    def out_part(down):
        return matmul(hidden, down).astype(jnp.bfloat16)

    def grad_part(gate, up):
        result = transposed(grad_gate, gate) + transposed(grad_up, up)
        return result.astype(jnp.bfloat16)

    def reduced(own, far):
        def piece(t):
            found = []
            for j in range(features // width):
                index = t * (features // width) + j
                at = (index // CORES ^ chip) * width
                here, there = (
                    lax.dynamic_slice_in_dim(side, at, width, axis=1) for side in (own, far)
                )
                found.append(jnp.where(index % CORES == core, here, there))
            return jnp.concatenate(found, axis=1)

        total = piece(tensor).astype(jnp.float32)
        for s in range(1, tensors):
            total += to_tensor(piece(tensor ^ s), s).astype(jnp.float32)
        pieces = total.reshape(half, 2, rows // 2, features)

        def chunk(z):
            return pieces[z % half, z // half]

        total = chunk(chip)
        for s in range(1, chips):
            sent = chunk(chip ^ s).astype(jnp.bfloat16)
            total += to_chip(sent, s).astype(jnp.float32)
        return total.astype(jnp.bfloat16)

    out_rows = reduced(out_part(down_own), out_part(down_far))
    grad_rows = reduced(grad_part(gate_own, up_own), grad_part(gate_far, up_far))

    is_lower = chip < half
    first = jnp.where(is_lower, 0, blocks - counts[me])

    def home(done):
        other = to_chip(done, half)
        pair = jnp.where(
            is_lower, jnp.concatenate([done, other]), jnp.concatenate([other, done])
        ).reshape(blocks, BLOCK, features)
        mine = jnp.take(pair, jnp.minimum(first + slot, blocks - 1), axis=0)
        mine = jnp.where((slot < counts[me])[:, None, None], mine, jnp.zeros_like(mine))
        return mine.reshape(rows, features)

    return home(out_rows), home(grad_rows)


def solution(mesh):
    in_specs = (
        P("dp", "tensor"),
        P("dp", "tensor"),
        P("dp", "tensor"),
        P("dp", "tensor"),
        P("tensor", "dp"),
        P(),
    )
    out_specs = (P("dp", "tensor"), P("dp", "tensor"))
    return jax.shard_map(
        per_device, mesh=mesh, in_specs=in_specs, out_specs=out_specs, check_vma=False
    )
```

```python
import functools

import jax
import jax.numpy as jnp
from jax import lax
from jax.experimental import pallas as pl
from jax.experimental.pallas import tpu as pltpu
from jax.sharding import PartitionSpec as P

BLOCK = 16
CORES = 2


def transposed(left, right):
    return lax.dot_general(
        left, right, (((1,), (1,)), ((), ())), preferred_element_type=jnp.float32
    )


def matmul(left, right):
    return jnp.dot(left, right, preferred_element_type=jnp.float32)


def spread_kernel(sizes, rows, gate, up, *refs):
    chips, tensors, part, width = sizes
    rows_all, own, far = refs[0], refs[1:3], refs[3:5]
    send, recv, local = refs[5:]
    me = lax.axis_index("dp")
    tensor = lax.axis_index("tensor")
    core, chip = me % CORES, me // CORES
    sibling = (me + 1 - 2 * core, tensor)

    def xored(value, step, size):
        result, bit = 0, 1
        while bit < size:
            digit = value // bit % 2
            result += (1 - digit if step & bit else digit) * bit
            bit *= 2
        return result

    def chip_of(step):
        return xored(chip, step, chips)

    def at_chip(step):
        return (chip_of(step) * CORES + core, tensor)

    def at_tensor(step):
        return (me, xored(tensor, step, tensors))

    steps = list(range(chips // 2, chips)) + list(range(1, chips // 2))
    peers = [at_chip(s) for s in steps] + [at_tensor(j) for j in range(1, tensors)] + [sibling]
    barrier = pltpu.get_barrier_semaphore()
    for peer in peers:
        pl.semaphore_signal(
            barrier, inc=1, device_id=peer, device_id_type=pl.DeviceIdType.MESH
        )
    pl.semaphore_wait(barrier, len(peers))

    started = []

    def put(source, target, device):
        n = len(started)
        copy = pltpu.make_async_remote_copy(
            src_ref=source,
            dst_ref=target,
            send_sem=send.at[n],
            recv_sem=recv.at[n],
            device_id=device,
            device_id_type=pl.DeviceIdType.MESH,
        )
        copy.start()
        started.append(copy)
        return copy

    def cut(ref, z):
        if len(ref.shape) == 3:
            return ref.at[z]
        return ref.at[:, pl.ds(pl.multiple_of(z * part, part), part)]

    weights = [(gate, own[0], far[0]), (up, own[1], far[1])]
    arriving_rows = [(s, put(rows, rows_all.at[0, s], at_chip(s))) for s in steps]
    arriving = []
    for weight, mine, other in weights:
        for s in steps:
            copy = put(cut(weight, chip_of(s)), mine.at[s], at_chip(s))
            arriving.append((copy, mine.at[s], other.at[s]))
    here = [pltpu.make_async_copy(rows, rows_all.at[0, 0], local.at[0])]
    last = []
    for j in range(1, tensors):
        last.append(put(rows, rows_all.at[j, 0], at_tensor(j)))
    for n, (weight, mine, other) in enumerate(weights):
        piece = cut(weight, chip)
        here.append(pltpu.make_async_copy(piece, mine.at[0], local.at[n + 1]))
        last.append(put(piece, other.at[0], sibling))
    for copy in here:
        copy.start()
    for s, copy in arriving_rows:
        copy.wait_recv()
        for j in range(1, tensors):
            last.append(put(rows_all.at[0, s], rows_all.at[j, s], at_tensor(j)))
    for copy, mine, other in arriving:
        copy.wait_recv()
        last.append(put(mine, other, sibling))
    for copy in last:
        copy.wait_recv()
    for copy in started:
        copy.wait_send()
    for copy in here:
        copy.wait()


def spread(rows, gate, up, sizes):
    chips, tensors, part, width = sizes
    kind = gate.dtype
    side = jax.ShapeDtypeStruct((chips, width, part), kind)
    copies = 3 * (chips - 1) + chips * (tensors - 1) + 2 * chips
    anywhere = pl.BlockSpec(memory_space=pl.ANY)
    return pl.pallas_call(
        functools.partial(spread_kernel, sizes),
        out_shape=[
            jax.ShapeDtypeStruct((tensors, chips) + rows.shape, kind),
            side, side, side, side,
        ],
        in_specs=[anywhere] * 3,
        out_specs=[anywhere] * 5,
        scratch_shapes=[
            pltpu.SemaphoreType.DMA((copies,)),
            pltpu.SemaphoreType.DMA((copies,)),
            pltpu.SemaphoreType.DMA((3,)),
        ],
        compiler_params=pltpu.CompilerParams(collective_id=0, has_side_effects=True),
    )(rows, gate, up)


def per_device(tokens, cotangent, gate_weight, up_weight, down_weight, counts):
    ranks = lax.axis_size("dp")
    tensors = lax.axis_size("tensor")
    chips = ranks // CORES
    half = chips // 2
    me = lax.axis_index("dp")
    core = me % CORES
    chip = me // CORES
    rows, features = tokens.shape
    blocks = rows // BLOCK
    width, units = gate_weight.shape
    part = units // chips
    tensor = lax.axis_index("tensor")

    def to_chip(block, step):
        route = [(i, (i // CORES ^ step) * CORES + i % CORES) for i in range(ranks)]
        return lax.ppermute(block, "dp", route)

    def swapped(block):
        return lax.ppermute(block, "dp", [(i, i ^ 1) for i in range(ranks)])

    def to_tensor(block, step):
        return lax.ppermute(block, "tensor", [(i, i ^ step) for i in range(tensors)])

    def pieces_of(weight):
        if part % 128 == 0:
            return weight
        return weight.reshape(width, chips, part).transpose(1, 0, 2)

    both = jnp.concatenate([tokens, cotangent], axis=1)
    raw, gate_own, up_own, gate_far, up_far = spread(
        both, pieces_of(gate_weight), pieces_of(up_weight), (chips, tensors, part, width)
    )
    down_weight, raw = lax.optimization_barrier((down_weight, raw))

    def down_rows(z):
        return lax.dynamic_slice_in_dim(down_weight, z * part, part, axis=0)

    down_pieces = [to_chip(down_rows(chip ^ s), s) for s in range(1, chips)]
    gate_own, up_own, gate_far, up_far = (
        w.reshape(chips * width, part) for w in (gate_own, up_own, gate_far, up_far)
    )

    slot = jnp.arange(blocks, dtype=jnp.int32)
    lower = jnp.arange(half, dtype=jnp.int32)
    lower_count = counts[lower * CORES + core][:, None]
    source = jnp.where(
        slot[None] < lower_count,
        jnp.bitwise_xor(lower[:, None], chip) * blocks + slot[None],
        jnp.bitwise_xor(lower[:, None] + half, chip) * blocks + slot[None] - lower_count,
    ).reshape(-1)
    work = half * rows
    raw = raw.reshape(tensors, chips * blocks, BLOCK, 2 * features)
    packed = jnp.take(raw, source, axis=1).reshape(tensors, work, 2 * features)

    def slices(c, shift):
        found = []
        for s in range(chips):
            at = ((chip ^ s) * CORES + c) * width
            start = (at // features ^ tensor, 0, at % features + shift)
            found.append(lax.dynamic_slice(packed, start, (1, work, width))[0])
        return jnp.concatenate(found, axis=1)

    x_own, x_far = slices(core, 0), slices(1 - core, 0)
    dy_own, dy_far = slices(core, features), slices(1 - core, features)
    gate_pre = matmul(x_own, gate_own) + matmul(x_far, gate_far)
    up_pre = matmul(x_own, up_own) + matmul(x_far, up_far)
    sigmoid_gate = jax.nn.sigmoid(gate_pre)
    activated = gate_pre * sigmoid_gate
    hidden = (activated * up_pre).astype(jnp.bfloat16)
    down_pieces, hidden = lax.optimization_barrier((down_pieces, hidden))
    down_own = jnp.concatenate([down_rows(chip)] + list(down_pieces), axis=1)
    down_far = swapped(down_own)
    grad_hidden = transposed(dy_own, down_own) + transposed(dy_far, down_far)
    grad_gate = (
        grad_hidden * up_pre * sigmoid_gate * (1.0 + gate_pre * (1.0 - sigmoid_gate))
    ).astype(jnp.bfloat16)
    grad_up = (grad_hidden * activated).astype(jnp.bfloat16)

    def out_part(down):
        return matmul(hidden, down).astype(jnp.bfloat16)

    def grad_part(gate, up):
        result = transposed(grad_gate, gate) + transposed(grad_up, up)
        return result.astype(jnp.bfloat16)

    def reduced(own, far):
        def piece(t):
            found = []
            for j in range(features // width):
                index = t * (features // width) + j
                at = (index // CORES ^ chip) * width
                here, there = (
                    lax.dynamic_slice_in_dim(side, at, width, axis=1) for side in (own, far)
                )
                found.append(jnp.where(index % CORES == core, here, there))
            return jnp.concatenate(found, axis=1)

        total = piece(tensor).astype(jnp.float32)
        for s in range(1, tensors):
            total += to_tensor(piece(tensor ^ s), s).astype(jnp.float32)
        pieces = total.reshape(half, rows, features)

        def chunk(z):
            return pieces[z % half]

        total = chunk(chip)
        for s in range(1, chips):
            sent = chunk(chip ^ s).astype(jnp.bfloat16)
            total += to_chip(sent, s).astype(jnp.float32)
        return total.astype(jnp.bfloat16)

    out_rows = reduced(out_part(down_own), out_part(down_far))
    grad_rows = reduced(grad_part(gate_own, up_own), grad_part(gate_far, up_far))

    is_lower = chip < half
    first = jnp.where(is_lower, 0, blocks - counts[me])

    def home(pair):
        pair = pair.reshape(blocks, BLOCK, features)
        mine = jnp.take(pair, jnp.minimum(first + slot, blocks - 1), axis=0)
        mine = jnp.where((slot < counts[me])[:, None, None], mine, jnp.zeros_like(mine))
        return mine.reshape(rows, features)

    return home(out_rows), home(grad_rows)


def solution(mesh):
    in_specs = (
        P("dp", "tensor"),
        P("dp", "tensor"),
        P("dp", "tensor"),
        P("dp", "tensor"),
        P("tensor", "dp"),
        P(),
    )
    out_specs = (P("dp", "tensor"), P("dp", "tensor"))
    return jax.shard_map(
        per_device, mesh=mesh, in_specs=in_specs, out_specs=out_specs, check_vma=False
    )
```
